256 devices in a mesh: row: 16 (over y_lo, x, core), col: 16 (over y_hi, z).
Axes of the slice: x: 4, y: 4 (y_hi: 2, y_lo: 2; y = y_hi * 2 + y_lo), z: 8, core: 2. Of those that a mesh axis runs over, the one named last changes fastest.
Arguments:
- val_orb: bfloat16 [64, 2048], replicated, may hold values from -6 to 6
- con_orb: bfloat16 [512, 2048], replicated, may hold values from -6 to 6
- val_energy: float32 [64], replicated, may hold values from -1.5 to -0.5
- con_energy: float32 [512], replicated, may hold values from 0.5 to 2
- points: int32 [1024], replicated, may hold values from 0 to 2047, as said below
- val_band: int32 [1048576], P(('row', 'col')), may hold values from 0 to 63
- con_band: int32 [1048576], P(('row', 'col')), may hold values from 0 to 511
- kernel: bfloat16 [1024, 1024], replicated
- trial_vecs: bfloat16 [1048576, 128], P(('row', 'col')), may hold values from -6 to 6
Outputs:
- first_degree: bfloat16 [1048576, 128], P(('row', 'col'))
- filtered: float32 [1048576, 128], P(('row', 'col'))
The draws below stay inside these ranges and needn't reach their ends.
Inputs may be any that keep to these rules, and one draw needn't show every extreme that they name: Distinct grid points.
All inputs are finite; a program needn't handle non-finite values.
Results may differ from the reference program's by a relative error of at most 0.0042.
Values sent between devices are 32-bit elements; how exact they have to be, the bound alone decides.
A program may use at most 128 MiB of HBM per device.

```python
import math
import jax
import jax.numpy as jnp
from jax import lax

NMU = 1024
NVEC = 128
NV = 64
NC = 512
NGRID = 2048
NPAIR = 1048576


def draw_points(key, part):
    return jax.random.permutation(key, NGRID)[:NMU].astype(jnp.int32)


def draw_kernel(key, part):
    key_one = jax.random.fold_in(key, 11)
    key_two = jax.random.fold_in(key, 12)
    square = jax.random.normal(key_one, (NMU, NMU), jnp.float32)
    symmetric = 0.5 * (square + square.T)
    diag_part = jax.random.uniform(key_two, (NMU,), jnp.float32, 1.0, 3.0) * NMU ** 0.5
    whole = symmetric + jnp.diag(diag_part)
    scale_all = 2.0 / (NMU ** 0.5 * NPAIR)
    return (whole * scale_all).astype(jnp.bfloat16)


def place_ends(entries, own_key, smallest, largest):
    longest = entries.shape.index(max(entries.shape))
    spots = []
    for shift in (0, 1):
        where = [jax.random.randint(jax.random.fold_in(own_key, axis), (), 0, length) for axis, length in enumerate(entries.shape)]
        where[longest] = (where[longest] + shift) % entries.shape[longest]
        spots.append(tuple(where))
    return entries.at[spots[0]].set(smallest).at[spots[1]].set(largest)


def block_scale(own_key, shape, pieces, smallest, high):
    loudness, own = 1.0, jax.random.fold_in(own_key, 6)
    for dim, shards_of in pieces:
        steps = jnp.exp(jax.random.uniform(jax.random.fold_in(own, dim), (shards_of,), jnp.float32, smallest / len(pieces), high / len(pieces)))
        loudness = loudness * jnp.repeat(steps, shape[dim] // shards_of).reshape([-1 if axis == dim else 1 for axis in range(len(shape))])
    return loudness


def noise(stream_key, shape, scale, reach, cuts=(), dtype=jnp.bfloat16):
    drawn = jax.random.normal(stream_key, shape, jnp.float32) * scale
    if len(cuts) > 0:
        drawn = block_scale(stream_key, shape, cuts, -0.22, 0.18) * drawn
    return jnp.clip(drawn, min=-reach, max=reach).astype(dtype)


def setup_inputs(seed: int = 0) -> dict:
    splits = jax.random.split(jax.random.key(seed), 10)
    val_orb = noise(splits[0], (NV, NGRID), 1.0, 6.0)
    con_orb = noise(splits[1], (NC, NGRID), 1.0, 6.0)
    val_energy = jnp.clip(jax.random.uniform(splits[2], (NV,), jnp.float32, -1.5, -0.5), -1.5, -0.5)
    con_energy = jnp.clip(jax.random.uniform(splits[3], (NC,), jnp.float32, 0.5, 2.0), 0.5, 2.0)
    points = draw_points(jax.random.fold_in(splits[9], 71), 0)
    val_band = place_ends(jax.random.randint(splits[5], (NPAIR,), 0, NV), jax.random.fold_in(splits[5], 1), 0, NV - 1).astype(jnp.int32)
    con_band = place_ends(jax.random.randint(splits[6], (NPAIR,), 0, NC), jax.random.fold_in(splits[6], 1), 0, NC - 1).astype(jnp.int32)
    kernel = draw_kernel(jax.random.fold_in(splits[9], 71), 0)
    trial_vecs = noise(splits[8], (NPAIR, NVEC), 1.0, 6.0, ((0, 256),))
    return dict(val_orb=val_orb, con_orb=con_orb, val_energy=val_energy, con_energy=con_energy, points=points, val_band=val_band, con_band=con_band, kernel=kernel, trial_vecs=trial_vecs)


filter_center = 2.25
filter_half = 1.25


def factor_rows(val_points, con_points, val_band, con_band):
    product = jnp.take(val_points, val_band, axis=0).astype(jnp.float32) * jnp.take(con_points, con_band, axis=0).astype(jnp.float32)
    return product.astype(jnp.bfloat16)


def reference(val_orb, con_orb, val_energy, con_energy, points, val_band, con_band, kernel, trial_vecs):
    block = math.gcd(NPAIR, 16384)
    blocks = NPAIR // block
    val_points = jnp.take(val_orb, points, axis=1)
    con_points = jnp.take(con_orb, points, axis=1)
    val_blocks = val_band.reshape(blocks, block)
    con_blocks = con_band.reshape(blocks, block)
    energy = (jnp.take(con_energy, con_band) - jnp.take(val_energy, val_band))[:, None]
    kernel_wide = kernel.astype(jnp.float32)

    def apply_kernel(vectors):
        vec_blocks = vectors.reshape(blocks, block, NVEC)

        def accumulate(total, items):
            rows = factor_rows(val_points, con_points, items[0], items[1])
            term = lax.dot_general(rows, items[2], (((0,), (0,)), ((), ())), preferred_element_type=jnp.float32)
            return total + term, None

        projected, unused = lax.scan(accumulate, jnp.zeros((NMU, NVEC), jnp.float32), (val_blocks, con_blocks, vec_blocks))
        mixed = jnp.dot(kernel_wide, projected, precision=lax.Precision.HIGHEST)

        def expand(items):
            rows = factor_rows(val_points, con_points, items[0], items[1])
            return jnp.dot(rows.astype(jnp.float32), mixed, precision=lax.Precision.HIGHEST)

        return lax.map(expand, (val_blocks, con_blocks)).reshape(NPAIR, NVEC)

    start_vecs = trial_vecs.astype(jnp.float32)
    first = ((energy - filter_center) * start_vecs + apply_kernel(trial_vecs)) / filter_half
    first_degree = first.astype(jnp.bfloat16)
    first_wide = first_degree.astype(jnp.float32)
    filtered = 2.0 * ((energy - filter_center) * first_wide + apply_kernel(first_degree)) / filter_half - start_vecs
    return first_degree, filtered
```

```python
import jax
import jax.numpy as jnp
from jax import lax
from jax.experimental import pallas as pl
from jax.experimental.pallas import tpu as pltpu
from jax.sharding import PartitionSpec as P

filter_center = 2.25
filter_half = 1.25

F32 = jnp.float32
BF16 = jnp.bfloat16
MESH = pl.DeviceIdType.MESH

NMU, NVEC, NV, NC, NGRID = 1024, 128, 64, 512, 2048
PAIRS = 4096
NB = 4
MB = NMU // NB
PC = 512
NPC = PAIRS // PC

CORE, PLANE, DEPTH, GATHER, JOIN = range(5)
PLANE_STEPS = sorted(
    range(1, 16), key=lambda d: -(min(d // 4, 4 - d // 4) + min(d % 4, 4 - d % 4))
)
DEPTH_STEPS = sorted(range(1, 8), key=lambda d: -min(d, 8 - d))


def dot(a, b):
    return jnp.dot(a, b, preferred_element_type=F32)


def dot_tn(a, b):
    return lax.dot_general(a, b, (((0,), (0,)), ((), ())), preferred_element_type=F32)


def halves(wide):
    high = wide.astype(BF16)
    low = (wide - high.astype(F32)).astype(BF16)
    return high, low


class Place:
    def __init__(self):
        row, col = lax.axis_index("row"), lax.axis_index("col")
        self.core = lax.rem(row, 2)
        self.x = lax.rem(lax.div(row, 2), 4)
        self.y = lax.div(col, 8) * 2 + lax.div(row, 8)
        self.z = lax.rem(col, 8)

    def at(self, x, y, z, core):
        row = (lax.rem(y, 2) * 4 + x) * 2 + core
        col = lax.div(y, 2) * 8 + z
        return (row, col)

    def partner(self):
        return self.at(self.x, self.y, self.z, 1 - self.core)

    def plane(self, d):
        x = lax.rem(self.x + d % 4, 4)
        y = lax.rem(self.y + d // 4, 4)
        return self.at(x, y, self.z, self.core)

    def depth(self, d):
        return self.at(self.x, self.y, lax.rem(self.z + d, 8), self.core)

    def everyone(self):
        return (
            [self.partner()]
            + [self.plane(d) for d in PLANE_STEPS]
            + [self.depth(d) for d in DEPTH_STEPS]
        )


class Sum:
    def __init__(self, place, part, core_in, half, plane_in, depth_in, whole, send, recv):
        self.p = place
        self.part, self.core_in, self.half = part, core_in, half
        self.plane_in, self.depth_in, self.whole = plane_in, depth_in, whole
        self.send, self.recv = send, recv
        self.slot = place.y * 4 + place.x
        self.owner = place.core * 16 + self.slot

    def copy(self, src, dst, stage, b, device):
        pltpu.make_async_remote_copy(
            src_ref=src,
            dst_ref=dst,
            send_sem=self.send.at[stage],
            recv_sem=self.recv.at[stage, b],
            device_id=device,
            device_id_type=MESH,
        ).start()

    def arrived(self, ref, stage, b):
        pltpu.make_async_copy(ref, ref, self.recv.at[stage, b]).wait()

    def sent(self, ref, stage):
        pltpu.make_async_copy(ref, ref, self.send.at[stage]).wait()

    def to_core(self, b):
        other = pl.multiple_of((1 - self.p.core) * 128, 128)
        self.copy(self.part.at[b, pl.ds(other, 128)], self.core_in.at[b], CORE, b, self.p.partner())

    def to_plane(self, b):
        self.arrived(self.core_in.at[b], CORE, b)
        own = pl.multiple_of(self.p.core * 128, 128)
        both = self.part[b, pl.ds(own, 128), :] + self.core_in[b]
        self.half[b] = both.reshape(16, 8, NVEC)
        for d in PLANE_STEPS:
            x = lax.rem(self.p.x + d % 4, 4)
            y = lax.rem(self.p.y + d // 4, 4)
            self.copy(self.half.at[b, y * 4 + x], self.plane_in.at[b, d], PLANE, b, self.p.plane(d))

    def to_depth(self, b):
        self.arrived(self.plane_in.at[b, pl.ds(1, 15)], PLANE, b)
        total = self.half[b, self.slot]
        for d in range(1, 16):
            total = total + self.plane_in[b, d]
        self.depth_in[b, 0] = total
        for d in DEPTH_STEPS:
            self.copy(self.depth_in.at[b, 0], self.depth_in.at[b, d], DEPTH, b, self.p.depth(d))

    def to_gather(self, b):
        self.arrived(self.depth_in.at[b, pl.ds(1, 7)], DEPTH, b)
        total = self.depth_in[b, 0]
        for d in range(1, 8):
            total = total + self.depth_in[b, d]
        self.whole[b, self.owner] = total
        for d in PLANE_STEPS:
            piece = self.whole.at[b, self.owner]
            self.copy(piece, piece, GATHER, b, self.p.plane(d))

    def to_join(self, b):
        self.arrived(self.plane_in.at[b, pl.ds(1, 15)], GATHER, b)
        piece = self.whole.at[b, pl.ds(self.p.core * 16, 16)]
        self.copy(piece, piece, JOIN, b, self.p.partner())

    def done(self, b):
        self.arrived(self.whole.at[b, pl.ds(0, 16)], JOIN, b)

    def close(self):
        self.sent(self.core_in, CORE)
        self.sent(self.plane_in.at[:, pl.ds(1, 15)], PLANE)
        self.sent(self.depth_in.at[:, pl.ds(1, 7)], DEPTH)
        self.sent(self.plane_in.at[:, pl.ds(1, 15)], GATHER)
        self.sent(self.whole.at[:, pl.ds(0, 16)], JOIN)


def filter_kernel(
    val_hbm, con_hbm, val_energy, con_energy, points, val_band, con_band, kernel_hbm, trial_hbm,
    first_out, filtered_out,
    orb, con_hot, val_hot, grid_hot, points_rows, rows, trial, mix, shifted, mixed_pair,
    part1, core1, half1, plane1, depth1, whole1,
    part2, core2, half2, plane2, depth2, whole2,
    load_sem, send1, recv1, send2, recv2,
):
    place = Place()
    barrier = pltpu.get_barrier_semaphore()
    for device in place.everyone():
        pl.semaphore_signal(barrier, inc=1, device_id=device, device_id_type=MESH)

    con_load = pltpu.make_async_copy(con_hbm, orb.at[pl.ds(0, NC)], load_sem.at[0])
    val_load = pltpu.make_async_copy(val_hbm, orb.at[pl.ds(NC, NV)], load_sem.at[1])
    trial_load = pltpu.make_async_copy(trial_hbm, trial, load_sem.at[2])
    mix_load = pltpu.make_async_copy(kernel_hbm, mix, load_sem.at[3])
    for load in (con_load, val_load, trial_load, mix_load):
        load.start()

    def build_hot(j, carry):
        lanes = pl.ds(pl.multiple_of(j * 128, 128), 128)
        con_row = con_band[pl.ds(j, 1), :]
        val_row = val_band[pl.ds(j, 1), :]
        for t in range(NC // 128):
            ids = lax.broadcasted_iota(jnp.int32, (128, 128), 0) + t * 128
            con_hot[t * 128 : (t + 1) * 128, lanes] = jnp.where(ids == con_row, 1.0, 0.0).astype(BF16)
        ids = lax.broadcasted_iota(jnp.int32, (NV, 128), 0)
        val_hot[:, lanes] = jnp.where(ids == val_row, 1.0, 0.0).astype(BF16)
        return carry

    lax.fori_loop(0, PAIRS // 128, build_hot, 0)
    con_load.wait()
    val_load.wait()

    sum1 = Sum(place, part1, core1, half1, plane1, depth1, whole1, send1, recv1)
    sum2 = Sum(place, part2, core2, half2, plane2, depth2, whole2, send2, recv2)

    for b in range(NB):
        for j in range(MB // 128):
            row = points[b * (MB // 128) + j : b * (MB // 128) + j + 1, :]
            for t in range(NGRID // 128):
                ids = lax.broadcasted_iota(jnp.int32, (128, 128), 0) + t * 128
                grid_hot[t * 128 : (t + 1) * 128, j * 128 : (j + 1) * 128] = jnp.where(
                    ids == row, 1.0, 0.0
                ).astype(BF16)
        points_rows[...] = dot(orb[...], grid_hot[...]).astype(BF16)

        def make_rows(j, carry):
            cols = pl.ds(pl.multiple_of(j * PC, PC), PC)
            con_part = dot_tn(points_rows[:NC, :], con_hot[:, cols])
            val_part = dot_tn(points_rows[NC:, :], val_hot[:, cols])
            rows[b * MB : (b + 1) * MB, cols] = (con_part * val_part).astype(BF16)
            return carry

        lax.fori_loop(0, NPC, make_rows, 0)
        if b == 0:
            trial_load.wait()
        part1[b] = dot(rows[b * MB : (b + 1) * MB, :], trial[...])
        if b == 0:
            pl.semaphore_wait(barrier, 23)
        sum1.to_core(b)
        if b >= 1:
            sum1.to_plane(b - 1)
        if b >= 2:
            sum1.to_depth(b - 2)
        if b >= 3:
            sum1.to_gather(b - 3)

    sum1.to_plane(NB - 1)

    con_col = jnp.broadcast_to(con_energy[...], (128, NC)).T
    val_col = jnp.broadcast_to(val_energy[...], (128, NV)).T
    con_pair = jnp.concatenate(halves(con_col), axis=1)
    val_pair = jnp.concatenate(halves(-val_col), axis=1)

    def make_shifted(j, carry):
        cols = pl.ds(pl.multiple_of(j * PC, PC), PC)
        both = dot_tn(con_hot[:, cols], con_pair) + dot_tn(val_hot[:, cols], val_pair)
        shifted[cols, :] = (both[:, :NVEC] + both[:, NVEC:]) - filter_center
        return carry

    lax.fori_loop(0, NPC, make_shifted, 0)
    mix_load.wait()

    def drain(total, plane_from, gather_from):
        for b in range(plane_from, NB):
            total.to_depth(b)
        for b in range(gather_from, NB):
            total.to_gather(b)
        for b in range(NB):
            total.to_join(b)

    def mixed_of(total):
        for b in range(NB):
            total.done(b)
            high, low = halves(total.whole[b].reshape(MB, NVEC))
            mixed_pair[b * MB : (b + 1) * MB, :NVEC] = high
            mixed_pair[b * MB : (b + 1) * MB, NVEC:] = low
        both = dot(mix[...], mixed_pair[...])
        high, low = halves(both[:, :NVEC] + both[:, NVEC:])
        mixed_pair[:, :NVEC] = high
        mixed_pair[:, NVEC:] = low

    def expand(cols):
        both = dot_tn(rows[:, cols], mixed_pair[...])
        return both[:, :NVEC] + both[:, NVEC:]

    drain(sum1, NB - 2, NB - 3)
    mixed_of(sum1)

    def first_step(j, carry):
        cols = pl.ds(pl.multiple_of(j * PC, PC), PC)
        value = shifted[cols, :] * trial[cols, :].astype(F32) + expand(cols)
        first_out[cols, :] = (value * (1.0 / filter_half)).astype(BF16)
        return carry

    lax.fori_loop(0, NPC, first_step, 0)

    for b in range(NB):
        part2[b] = dot(rows[b * MB : (b + 1) * MB, :], first_out[...])
        sum2.to_core(b)
        if b >= 1:
            sum2.to_plane(b - 1)
    sum2.to_plane(NB - 1)
    drain(sum2, 0, 0)
    mixed_of(sum2)

    def second_step(j, carry):
        cols = pl.ds(pl.multiple_of(j * PC, PC), PC)
        value = shifted[cols, :] * first_out[cols, :].astype(F32) + expand(cols)
        filtered_out[cols, :] = value * (2.0 / filter_half) - trial[cols, :].astype(F32)
        return carry

    lax.fori_loop(0, NPC, second_step, 0)
    sum1.close()
    sum2.close()


def shards(
    val_orb, con_orb, val_energy, con_energy, points, val_band, con_band, kernel, trial_vecs
):
    vmem = pl.BlockSpec(memory_space=pltpu.VMEM)
    away = pl.BlockSpec(memory_space=pl.ANY)

    def sum_buffers():
        return [
            pltpu.VMEM((NB, MB, NVEC), F32),
            pltpu.VMEM((NB, 128, NVEC), F32),
            pltpu.VMEM((NB, 16, 8, NVEC), F32),
            pltpu.VMEM((NB, 16, 8, NVEC), F32),
            pltpu.VMEM((NB, 8, 8, NVEC), F32),
            pltpu.VMEM((NB, 32, 8, NVEC), F32),
        ]

    return pl.pallas_call(
        filter_kernel,
        out_shape=(
            jax.ShapeDtypeStruct((PAIRS, NVEC), BF16),
            jax.ShapeDtypeStruct((PAIRS, NVEC), F32),
        ),
        in_specs=[away, away, vmem, vmem, vmem, vmem, vmem, away, away],
        out_specs=(vmem, vmem),
        scratch_shapes=[
            pltpu.VMEM((NC + NV, NGRID), BF16),
            pltpu.VMEM((NC, PAIRS), BF16),
            pltpu.VMEM((NV, PAIRS), BF16),
            pltpu.VMEM((NGRID, MB), BF16),
            pltpu.VMEM((NC + NV, MB), BF16),
            pltpu.VMEM((NMU, PAIRS), BF16),
            pltpu.VMEM((PAIRS, NVEC), BF16),
            pltpu.VMEM((NMU, NMU), BF16),
            pltpu.VMEM((PAIRS, NVEC), F32),
            pltpu.VMEM((NMU, 2 * NVEC), BF16),
        ]
        + sum_buffers()
        + sum_buffers()
        + [
            pltpu.SemaphoreType.DMA((4,)),
            pltpu.SemaphoreType.DMA((5,)),
            pltpu.SemaphoreType.DMA((5, NB)),
            pltpu.SemaphoreType.DMA((5,)),
            pltpu.SemaphoreType.DMA((5, NB)),
        ],
        compiler_params=pltpu.CompilerParams(
            collective_id=0, has_side_effects=True, vmem_limit_bytes=48 * 1024 * 1024
        ),
    )(
        val_orb,
        con_orb,
        val_energy.reshape(1, NV),
        con_energy.reshape(1, NC),
        points.reshape(8, 128),
        val_band.reshape(PAIRS // 128, 128),
        con_band.reshape(PAIRS // 128, 128),
        kernel,
        trial_vecs,
    )


def solution(mesh):
    placed = (P(), P(), P(), P(), P(), P(("row", "col")), P(("row", "col")), P(), P(("row", "col"), None))
    return jax.shard_map(
        shards,
        mesh=mesh,
        in_specs=placed,
        out_specs=(P(("row", "col"), None), P(("row", "col"), None)),
        check_vma=False,
    )
```

```python
import jax
import jax.numpy as jnp
from jax import lax
from jax.experimental import pallas as pl
from jax.experimental.pallas import tpu as pltpu
from jax.sharding import PartitionSpec as P

filter_center = 2.25
filter_half = 1.25

F32 = jnp.float32
BF16 = jnp.bfloat16
MESH = pl.DeviceIdType.MESH

NMU, NVEC, NV, NC, NGRID = 1024, 128, 64, 512, 2048
PAIRS = 4096
NB = 4
MB = NMU // NB
PC = 512
NPC = PAIRS // PC

CORE, PLANE, DEPTH, GATHER, JOIN = range(5)
PLANE_STEPS = sorted(
    range(1, 16), key=lambda d: -(min(d // 4, 4 - d // 4) + min(d % 4, 4 - d % 4))
)
DEPTH_STEPS = sorted(range(1, 8), key=lambda d: -min(d, 8 - d))


def dot(a, b):
    return jnp.dot(a, b, preferred_element_type=F32)


def halves(wide):
    high = wide.astype(BF16)
    low = (wide - high.astype(F32)).astype(BF16)
    return high, low


class Place:
    def __init__(self):
        row, col = lax.axis_index("row"), lax.axis_index("col")
        self.core = lax.rem(row, 2)
        self.x = lax.rem(lax.div(row, 2), 4)
        self.y = lax.div(col, 8) * 2 + lax.div(row, 8)
        self.z = lax.rem(col, 8)

    def at(self, x, y, z, core):
        row = (lax.rem(y, 2) * 4 + x) * 2 + core
        col = lax.div(y, 2) * 8 + z
        return (row, col)

    def partner(self):
        return self.at(self.x, self.y, self.z, 1 - self.core)

    def plane(self, d):
        x = lax.rem(self.x + d % 4, 4)
        y = lax.rem(self.y + d // 4, 4)
        return self.at(x, y, self.z, self.core)

    def depth(self, d):
        return self.at(self.x, self.y, lax.rem(self.z + d, 8), self.core)

    def everyone(self):
        return (
            [self.partner()]
            + [self.plane(d) for d in PLANE_STEPS]
            + [self.depth(d) for d in DEPTH_STEPS]
        )


class Sum:
    def __init__(self, place, part, core_in, half, plane_in, depth_in, whole, send, recv):
        self.p = place
        self.part, self.core_in, self.half = part, core_in, half
        self.plane_in, self.depth_in, self.whole = plane_in, depth_in, whole
        self.send, self.recv = send, recv
        self.slot = place.y * 4 + place.x
        self.owner = place.core * 16 + self.slot

    def copy(self, src, dst, stage, b, device):
        pltpu.make_async_remote_copy(
            src_ref=src,
            dst_ref=dst,
            send_sem=self.send.at[stage],
            recv_sem=self.recv.at[stage, b],
            device_id=device,
            device_id_type=MESH,
        ).start()

    def arrived(self, ref, stage, b):
        pltpu.make_async_copy(ref, ref, self.recv.at[stage, b]).wait()

    def sent(self, ref, stage):
        pltpu.make_async_copy(ref, ref, self.send.at[stage]).wait()

    def to_core(self, b):
        other = pl.multiple_of((1 - self.p.core) * 128, 128)
        self.copy(self.part.at[b, pl.ds(other, 128)], self.core_in.at[b], CORE, b, self.p.partner())

    def to_plane(self, b):
        self.arrived(self.core_in.at[b], CORE, b)
        own = pl.multiple_of(self.p.core * 128, 128)
        both = self.part[b, pl.ds(own, 128), :] + self.core_in[b]
        self.half[b] = both.reshape(16, 8, NVEC)
        for d in PLANE_STEPS:
            x = lax.rem(self.p.x + d % 4, 4)
            y = lax.rem(self.p.y + d // 4, 4)
            self.copy(self.half.at[b, y * 4 + x], self.plane_in.at[b, d], PLANE, b, self.p.plane(d))

    def to_depth(self, b):
        self.arrived(self.plane_in.at[b, pl.ds(1, 15)], PLANE, b)
        total = self.half[b, self.slot]
        for d in range(1, 16):
            total = total + self.plane_in[b, d]
        self.depth_in[b, 0] = total
        for d in DEPTH_STEPS:
            self.copy(self.depth_in.at[b, 0], self.depth_in.at[b, d], DEPTH, b, self.p.depth(d))

    def to_gather(self, b):
        self.arrived(self.depth_in.at[b, pl.ds(1, 7)], DEPTH, b)
        total = self.depth_in[b, 0]
        for d in range(1, 8):
            total = total + self.depth_in[b, d]
        self.whole[b, self.owner] = total
        for d in PLANE_STEPS:
            piece = self.whole.at[b, self.owner]
            self.copy(piece, piece, GATHER, b, self.p.plane(d))

    def to_join(self, b):
        self.arrived(self.plane_in.at[b, pl.ds(1, 15)], GATHER, b)
        piece = self.whole.at[b, pl.ds(self.p.core * 16, 16)]
        self.copy(piece, piece, JOIN, b, self.p.partner())

    def done(self, b):
        self.arrived(self.whole.at[b, pl.ds(0, 16)], JOIN, b)

    def close(self):
        self.sent(self.core_in, CORE)
        self.sent(self.plane_in.at[:, pl.ds(1, 15)], PLANE)
        self.sent(self.depth_in.at[:, pl.ds(1, 7)], DEPTH)
        self.sent(self.plane_in.at[:, pl.ds(1, 15)], GATHER)
        self.sent(self.whole.at[:, pl.ds(0, 16)], JOIN)


def filter_kernel(
    val_hbm, con_hbm, val_energy_hbm, con_energy_hbm, points_hbm, val_band_hbm, con_band_hbm,
    kernel_hbm, trial_hbm,
    first_out, filtered_out,
    val_energy, con_energy, points, val_band, con_band,
    orb, con_hot, val_hot, grid_hot, points_rows, rows, trial, turned, mix, shifted, mixed_pair,
    part1, core1, half1, plane1, depth1, whole1,
    part2, core2, half2, plane2, depth2, whole2,
    load_sem, send1, recv1, send2, recv2,
):
    def load(src, dst, k):
        copy = pltpu.make_async_copy(src, dst, load_sem.at[k])
        copy.start()
        return copy

    points_load = load(points_hbm, points, 0)
    con_band_load = load(con_band_hbm, con_band, 1)
    val_band_load = load(val_band_hbm, val_band, 2)
    con_load = load(con_hbm, orb.at[pl.ds(0, NC)], 3)
    val_load = load(val_hbm, orb.at[pl.ds(NC, NV)], 4)
    trial_load = load(trial_hbm, trial, 5)
    con_energy_load = load(con_energy_hbm, con_energy, 6)
    val_energy_load = load(val_energy_hbm, val_energy, 7)
    mix_load = load(kernel_hbm, mix, 8)

    place = Place()
    barrier = pltpu.get_barrier_semaphore()
    for device in place.everyone():
        pl.semaphore_signal(barrier, inc=1, device_id=device, device_id_type=MESH)

    def build_grid(b, t):
        ids = lax.broadcasted_iota(jnp.int32, (128, 128), 0) + t * 128
        for j in range(MB // 128):
            k = b * (MB // 128) + j
            grid_hot[b % 2, pl.ds(pl.multiple_of(t * 128, 128), 128), j * 128 : (j + 1) * 128] = jnp.where(
                ids == points[k : k + 1, :], 1.0, 0.0
            ).astype(BF16)

    points_load.wait()
    for t in range(NGRID // 128):
        build_grid(0, t)
    con_band_load.wait()
    val_band_load.wait()

    def build_hot(j, carry):
        both = (con_band[pl.ds(j, 1), :] * NV + val_band[pl.ds(j, 1), :]).astype(F32)
        column = jnp.broadcast_to(both, (128, 128)).T.astype(jnp.int32)
        con_column = lax.shift_right_logical(column, 6)
        val_column = lax.bitwise_and(column, NV - 1)
        ids = lax.broadcasted_iota(jnp.int32, (128, 128), 1)
        pairs = pl.ds(pl.multiple_of(j * 128, 128), 128)
        for t in range(NC // 128):
            con_hot[pairs, t * 128 : (t + 1) * 128] = jnp.where(ids + t * 128 == con_column, 1.0, 0.0).astype(BF16)
        val_hot[pairs, :] = jnp.where(ids == val_column, 1.0, 0.0).astype(BF16)
        return carry

    lax.fori_loop(0, PAIRS // 128, build_hot, 0)
    con_load.wait()
    val_load.wait()
    trial_load.wait()

    sum1 = Sum(place, part1, core1, half1, plane1, depth1, whole1, send1, recv1)
    sum2 = Sum(place, part2, core2, half2, plane2, depth2, whole2, send2, recv2)

    def project(total, b):
        both = dot(turned[...], rows[:, b * MB : (b + 1) * MB])
        total.part[b, :128, :] = both[:, :128]
        total.part[b, 128:, :] = both[:, 128:]

    points_rows[NC + NV :, :] = jnp.zeros((128 - NV, MB), BF16)
    for b in range(NB):
        points_rows[: NC + NV, :] = dot(orb[...], grid_hot[b % 2]).astype(BF16)

        def make_rows(j, carry):
            chunk = pl.ds(pl.multiple_of(j * PC, PC), PC)
            con_part = dot(con_hot[chunk, :], points_rows[:NC, :])
            val_part = dot(val_hot[chunk, :], points_rows[NC:, :])
            rows[chunk, b * MB : (b + 1) * MB] = (con_part * val_part).astype(BF16)
            if b == 0:
                turned[:, chunk] = trial[chunk, :].astype(F32).T.astype(BF16)
            if b + 1 < NB:
                for t in range(NGRID // 128 // NPC):
                    build_grid(b + 1, j * (NGRID // 128 // NPC) + t)
            return carry

        lax.fori_loop(0, NPC, make_rows, 0)
        project(sum1, b)
        if b == 0:
            pl.semaphore_wait(barrier, 23)
        sum1.to_core(b)
        if b >= 1:
            sum1.to_plane(b - 1)
        if b >= 2:
            sum1.to_depth(b - 2)
        if b >= 3:
            sum1.to_gather(b - 3)

    sum1.to_plane(NB - 1)
    con_energy_load.wait()
    val_energy_load.wait()
    con_col = jnp.broadcast_to(con_energy[...], (128, NC)).T
    val_col = jnp.broadcast_to(val_energy[...], (128, NV)).T
    con_pair = jnp.concatenate(halves(con_col), axis=1)
    val_pair = jnp.concatenate(halves(-val_col), axis=1)

    def make_shifted(j, carry):
        chunk = pl.ds(pl.multiple_of(j * PC, PC), PC)
        both = dot(con_hot[chunk, :], con_pair) + dot(val_hot[chunk, :NV], val_pair)
        shifted[chunk, :] = (both[:, :NVEC] + both[:, NVEC:]) - filter_center
        return carry

    lax.fori_loop(0, NPC, make_shifted, 0)
    mix_load.wait()

    def drain(total, plane_from, gather_from):
        for b in range(plane_from, NB):
            total.to_depth(b)
        for b in range(gather_from, NB):
            total.to_gather(b)
        for b in range(NB):
            total.to_join(b)

    def mixed_of(total):
        for b in range(NB):
            total.done(b)
            for h in range(2):
                at = b * MB + h * 128
                piece = total.whole[b, h * 16 : (h + 1) * 16].reshape(NVEC, 128).T
                high, low = halves(piece)
                mixed_pair[at : at + 128, :NVEC] = high
                mixed_pair[at : at + 128, NVEC:] = low
        both = dot(mix[...], mixed_pair[...])
        high, low = halves(both[:, :NVEC] + both[:, NVEC:])
        mixed_pair[:, :NVEC] = high
        mixed_pair[:, NVEC:] = low

    def expand(chunk):
        both = dot(rows[chunk, :], mixed_pair[...])
        return both[:, :NVEC] + both[:, NVEC:]

    drain(sum1, NB - 2, NB - 3)
    mixed_of(sum1)

    def first_step(j, carry):
        chunk = pl.ds(pl.multiple_of(j * PC, PC), PC)
        value = shifted[chunk, :] * trial[chunk, :].astype(F32) + expand(chunk)
        rounded = (value * (1.0 / filter_half)).astype(BF16)
        first_out[chunk, :] = rounded
        turned[:, chunk] = rounded.astype(F32).T.astype(BF16)
        return carry

    lax.fori_loop(0, NPC, first_step, 0)

    for b in range(NB):
        project(sum2, b)
        sum2.to_core(b)
        if b >= 1:
            sum2.to_plane(b - 1)
    sum2.to_plane(NB - 1)
    drain(sum2, 0, 0)
    mixed_of(sum2)

    def second_step(j, carry):
        chunk = pl.ds(pl.multiple_of(j * PC, PC), PC)
        value = shifted[chunk, :] * first_out[chunk, :].astype(F32) + expand(chunk)
        filtered_out[chunk, :] = value * (2.0 / filter_half) - trial[chunk, :].astype(F32)
        return carry

    lax.fori_loop(0, NPC, second_step, 0)
    sum1.close()
    sum2.close()


def store_kernel(first_in, filtered_in, first_out, filtered_out, sem):
    copies = [
        pltpu.make_async_copy(first_in, first_out, sem.at[0]),
        pltpu.make_async_copy(filtered_in, filtered_out, sem.at[1]),
    ]
    for copy in copies:
        copy.start()
    for copy in copies:
        copy.wait()


def shards(
    val_orb, con_orb, val_energy, con_energy, points, val_band, con_band, kernel, trial_vecs
):
    vmem = pl.BlockSpec(memory_space=pltpu.VMEM)
    away = pl.BlockSpec(memory_space=pltpu.HBM)

    def sum_buffers():
        return [
            pltpu.VMEM((NB, MB, NVEC), F32),
            pltpu.VMEM((NB, 128, NVEC), F32),
            pltpu.VMEM((NB, 16, 8, NVEC), F32),
            pltpu.VMEM((NB, 16, 8, NVEC), F32),
            pltpu.VMEM((NB, 8, 8, NVEC), F32),
            pltpu.VMEM((NB, 32, 8, NVEC), F32),
        ]

    shapes = (
        jax.ShapeDtypeStruct((PAIRS, NVEC), BF16),
        jax.ShapeDtypeStruct((PAIRS, NVEC), F32),
    )
    first, filtered = pl.pallas_call(
        filter_kernel,
        out_shape=shapes,
        in_specs=[away] * 9,
        out_specs=(vmem, vmem),
        scratch_shapes=[
            pltpu.VMEM((1, NV), F32),
            pltpu.VMEM((1, NC), F32),
            pltpu.VMEM((8, 128), jnp.int32),
            pltpu.VMEM((PAIRS // 128, 128), jnp.int32),
            pltpu.VMEM((PAIRS // 128, 128), jnp.int32),
            pltpu.VMEM((NC + NV, NGRID), BF16),
            pltpu.VMEM((PAIRS, NC), BF16),
            pltpu.VMEM((PAIRS, 128), BF16),
            pltpu.VMEM((2, NGRID, MB), BF16),
            pltpu.VMEM((NC + 128, MB), BF16),
            pltpu.VMEM((PAIRS, NMU), BF16),
            pltpu.VMEM((PAIRS, NVEC), BF16),
            pltpu.VMEM((NVEC, PAIRS), BF16),
            pltpu.VMEM((NMU, NMU), BF16),
            pltpu.VMEM((PAIRS, NVEC), F32),
            pltpu.VMEM((NMU, 2 * NVEC), BF16),
        ]
        + sum_buffers()
        + sum_buffers()
        + [
            pltpu.SemaphoreType.DMA((9,)),
            pltpu.SemaphoreType.DMA((5,)),
            pltpu.SemaphoreType.DMA((5, NB)),
            pltpu.SemaphoreType.DMA((5,)),
            pltpu.SemaphoreType.DMA((5, NB)),
        ],
        compiler_params=pltpu.CompilerParams(
            collective_id=0, has_side_effects=True, vmem_limit_bytes=48 * 1024 * 1024
        ),
    )(
        *(
            pltpu.with_memory_space_constraint(value, pltpu.HBM)
            for value in (
                val_orb,
                con_orb,
                val_energy.reshape(1, NV),
                con_energy.reshape(1, NC),
                points.reshape(8, 128),
                val_band.reshape(PAIRS // 128, 128),
                con_band.reshape(PAIRS // 128, 128),
                kernel,
                trial_vecs,
            )
        )
    )
    return pl.pallas_call(
        store_kernel,
        out_shape=shapes,
        in_specs=[vmem, vmem],
        out_specs=(away, away),
        scratch_shapes=[pltpu.SemaphoreType.DMA((2,))],
        compiler_params=pltpu.CompilerParams(vmem_limit_bytes=1024 * 1024),
    )(first, filtered)


def solution(mesh):
    placed = (P(), P(), P(), P(), P(), P(("row", "col")), P(("row", "col")), P(), P(("row", "col"), None))
    return jax.shard_map(
        shards,
        mesh=mesh,
        in_specs=placed,
        out_specs=(P(("row", "col"), None), P(("row", "col"), None)),
        check_vma=False,
    )
```

```python
import jax
import jax.numpy as jnp
from jax import lax
from jax.experimental import pallas as pl
from jax.experimental.pallas import tpu as pltpu
from jax.sharding import PartitionSpec as P

filter_center = 2.25
filter_half = 1.25

F32 = jnp.float32
BF16 = jnp.bfloat16
MESH = pl.DeviceIdType.MESH

NMU, NVEC, NV, NC, NGRID = 1024, 128, 64, 512, 2048
PAIRS = 4096
NB = 4
MB = NMU // NB
NCB = 2
CB = NMU // NCB
PC = 512
NPC = PAIRS // PC
PR = 512
NPR = PAIRS // PR

CORE, PLANE, DEPTH, GATHER, JOIN = range(5)
PLANE_STEPS = sorted(
    range(1, 16), key=lambda d: -(min(d // 4, 4 - d // 4) + min(d % 4, 4 - d % 4))
)
DEPTH_STEPS = sorted(range(1, 8), key=lambda d: -min(d, 8 - d))


def dot(a, b):
    return jnp.dot(a, b, preferred_element_type=F32)


def halves(wide):
    high = wide.astype(BF16)
    low = (wide - high.astype(F32)).astype(BF16)
    return high, low


class Place:
    def __init__(self):
        row, col = lax.axis_index("row"), lax.axis_index("col")
        self.core = lax.rem(row, 2)
        self.x = lax.rem(lax.div(row, 2), 4)
        self.y = lax.div(col, 8) * 2 + lax.div(row, 8)
        self.z = lax.rem(col, 8)

    def at(self, x, y, z, core):
        row = (lax.rem(y, 2) * 4 + x) * 2 + core
        col = lax.div(y, 2) * 8 + z
        return (row, col)

    def partner(self):
        return self.at(self.x, self.y, self.z, 1 - self.core)

    def plane(self, d):
        x = lax.rem(self.x + d % 4, 4)
        y = lax.rem(self.y + d // 4, 4)
        return self.at(x, y, self.z, self.core)

    def depth(self, d):
        return self.at(self.x, self.y, lax.rem(self.z + d, 8), self.core)

    def everyone(self):
        return (
            [self.partner()]
            + [self.plane(d) for d in PLANE_STEPS]
            + [self.depth(d) for d in DEPTH_STEPS]
        )


class Sum:
    def __init__(self, place, part, core_in, half, plane_in, depth_in, whole, send, recv):
        self.p = place
        self.part, self.core_in, self.half = part, core_in, half
        self.plane_in, self.depth_in, self.whole = plane_in, depth_in, whole
        self.send, self.recv = send, recv
        self.slot = place.y * 4 + place.x
        self.owner = place.core * 16 + self.slot

    def copy(self, src, dst, stage, b, device):
        pltpu.make_async_remote_copy(
            src_ref=src,
            dst_ref=dst,
            send_sem=self.send.at[stage],
            recv_sem=self.recv.at[stage, b],
            device_id=device,
            device_id_type=MESH,
        ).start()

    def arrived(self, ref, stage, b):
        pltpu.make_async_copy(ref, ref, self.recv.at[stage, b]).wait()

    def sent(self, ref, stage):
        pltpu.make_async_copy(ref, ref, self.send.at[stage]).wait()

    def to_core(self, b):
        other = pl.multiple_of((1 - self.p.core) * 128, 128)
        self.copy(self.part.at[b, pl.ds(other, 128)], self.core_in.at[b], CORE, b, self.p.partner())

    def to_plane(self, b):
        self.arrived(self.core_in.at[b], CORE, b)
        own = pl.multiple_of(self.p.core * 128, 128)
        both = self.part[b, pl.ds(own, 128), :] + self.core_in[b]
        self.half[b] = both.reshape(16, 8, NVEC)
        for d in PLANE_STEPS:
            x = lax.rem(self.p.x + d % 4, 4)
            y = lax.rem(self.p.y + d // 4, 4)
            self.copy(self.half.at[b, y * 4 + x], self.plane_in.at[b, d], PLANE, b, self.p.plane(d))

    def to_depth(self, b):
        self.arrived(self.plane_in.at[b, pl.ds(1, 15)], PLANE, b)
        total = self.half[b, self.slot]
        for d in range(1, 16):
            total = total + self.plane_in[b, d]
        self.depth_in[b, 0] = total
        for d in DEPTH_STEPS:
            self.copy(self.depth_in.at[b, 0], self.depth_in.at[b, d], DEPTH, b, self.p.depth(d))

    def to_gather(self, b):
        self.arrived(self.depth_in.at[b, pl.ds(1, 7)], DEPTH, b)
        total = self.depth_in[b, 0]
        for d in range(1, 8):
            total = total + self.depth_in[b, d]
        self.whole[b, self.owner] = total
        for d in PLANE_STEPS:
            piece = self.whole.at[b, self.owner]
            self.copy(piece, piece, GATHER, b, self.p.plane(d))

    def to_join(self, b):
        self.arrived(self.plane_in.at[b, pl.ds(1, 15)], GATHER, b)
        piece = self.whole.at[b, pl.ds(self.p.core * 16, 16)]
        self.copy(piece, piece, JOIN, b, self.p.partner())

    def done(self, b):
        self.arrived(self.whole.at[b, pl.ds(0, 16)], JOIN, b)

    def close(self):
        self.sent(self.core_in, CORE)
        self.sent(self.plane_in.at[:, pl.ds(1, 15)], PLANE)
        self.sent(self.depth_in.at[:, pl.ds(1, 7)], DEPTH)
        self.sent(self.plane_in.at[:, pl.ds(1, 15)], GATHER)
        self.sent(self.whole.at[:, pl.ds(0, 16)], JOIN)


def filter_kernel(
    val_hbm, con_hbm, val_energy_hbm, con_energy_hbm, points_hbm, val_band_hbm, con_band_hbm,
    kernel_hbm, trial_hbm,
    first_out, filtered_out,
    val_energy, con_energy, points, val_band, con_band,
    orb, con_hot, val_hot, grid_hot, points_rows, rows, trial, turned, gathered, mix, shifted, mixed_pair,
    part1, core1, half1, plane1, depth1, whole1,
    part2, core2, half2, plane2, depth2, whole2,
    load_sem, send1, recv1, send2, recv2,
):
    def load(src, dst, k):
        copy = pltpu.make_async_copy(src, dst, load_sem.at[k])
        copy.start()
        return copy

    points_load = load(points_hbm, points, 0)
    con_band_load = load(con_band_hbm, con_band, 1)
    val_band_load = load(val_band_hbm, val_band, 2)
    con_load = load(con_hbm, orb.at[pl.ds(0, NC)], 3)
    val_load = load(val_hbm, orb.at[pl.ds(NC, NV)], 4)
    trial_load = load(trial_hbm, trial, 5)
    con_energy_load = load(con_energy_hbm, con_energy, 6)
    val_energy_load = load(val_energy_hbm, val_energy, 7)
    mix_load = load(kernel_hbm, mix, 8)

    place = Place()
    barrier = pltpu.get_barrier_semaphore()
    for device in place.everyone():
        pl.semaphore_signal(barrier, inc=1, device_id=device, device_id_type=MESH)

    def build_grid(b, t):
        ids = lax.broadcasted_iota(jnp.int32, (128, 128), 0) + t * 128
        for j in range(CB // 128):
            k = b * (CB // 128) + j
            grid_hot[b, pl.ds(pl.multiple_of(t * 128, 128), 128), j * 128 : (j + 1) * 128] = jnp.where(
                ids == points[k : k + 1, :], 1.0, 0.0
            ).astype(BF16)

    points_load.wait()
    for t in range(NGRID // 128):
        build_grid(0, t)
    con_band_load.wait()
    val_band_load.wait()

    def build_hot(j):
        both = (con_band[pl.ds(j, 1), :] * NV + val_band[pl.ds(j, 1), :]).astype(F32)
        column = jnp.broadcast_to(both, (128, 128)).T.astype(jnp.int32)
        con_column = lax.shift_right_logical(column, 6)
        val_column = lax.bitwise_and(column, NV - 1)
        ids = lax.broadcasted_iota(jnp.int32, (128, 128), 1)
        pairs = pl.ds(pl.multiple_of(j * 128, 128), 128)
        for t in range(NC // 128):
            con_hot[pairs, t * 128 : (t + 1) * 128] = jnp.where(ids + t * 128 == con_column, 1.0, 0.0).astype(BF16)
        val_hot[pairs, :] = jnp.where(ids == val_column, 1.0, 0.0).astype(BF16)

    def build_four(j, carry):
        for k in range(4):
            build_hot(4 * j + k)
        return carry

    lax.fori_loop(0, PAIRS // 512, build_four, 0)
    con_load.wait()
    val_load.wait()
    trial_load.wait()

    sum1 = Sum(place, part1, core1, half1, plane1, depth1, whole1, send1, recv1)
    sum2 = Sum(place, part2, core2, half2, plane2, depth2, whole2, send2, recv2)

    def project(chunk, lanes):
        return dot(turned[:, chunk], rows[chunk, lanes])

    def keep(total, first, value):
        for k in range(value.shape[1] // 128):
            b, h = first + k // 2, k % 2
            total.part[b, h * 128 : (h + 1) * 128, :] = value[:, k * 128 : (k + 1) * 128]

    points_rows[NC + NV :, :] = jnp.zeros((128 - NV, CB), BF16)
    for c in range(NCB):
        points_rows[: NC + NV, :] = dot(orb[...], grid_hot[c]).astype(BF16)
        if c == 0:
            for t in range(NGRID // 128):
                build_grid(1, t)
            for k in range(NPC):
                chunk = slice(k * PC, (k + 1) * PC)
                turned[:, chunk] = trial[chunk, :].astype(F32).T.astype(BF16)
        if c == 1:
            for b in range(NB // 2):
                sum1.to_plane(b)
        block = slice(c * CB, (c + 1) * CB)

        def make_rows(j, carry):
            chunk = pl.ds(pl.multiple_of(j * PR, PR), PR)
            before = pl.ds(pl.multiple_of(jnp.maximum(j - 1, 0) * PR, PR), PR)
            so_far = gathered[:, :CB] + project(before, block)
            gathered[:, :CB] = jnp.where(j > 0, so_far, 0.0)
            con_part = dot(con_hot[chunk, :], points_rows[:NC, :])
            val_part = dot(val_hot[chunk, :], points_rows[NC:, :])
            rows[chunk, block] = (con_part * val_part).astype(BF16)
            return carry

        lax.fori_loop(0, NPR, make_rows, 0)
        keep(sum1, c * 2, gathered[:, :CB] + project(slice(PAIRS - PR, PAIRS), block))
        if c == 0:
            pl.semaphore_wait(barrier, 23)
        sum1.to_core(c * 2)
        sum1.to_core(c * 2 + 1)

    for b in range(NB // 2):
        sum1.to_depth(b)
    for b in range(NB // 2, NB):
        sum1.to_plane(b)
    con_energy_load.wait()
    val_energy_load.wait()
    con_col = jnp.broadcast_to(con_energy[...], (128, NC)).T
    val_col = jnp.broadcast_to(val_energy[...], (128, NV)).T
    con_pair = jnp.concatenate(halves(con_col), axis=1)
    val_pair = jnp.concatenate(halves(-val_col), axis=1)

    def make_shifted(j, carry):
        chunk = pl.ds(pl.multiple_of(j * PC, PC), PC)
        both = dot(con_hot[chunk, :], con_pair) + dot(val_hot[chunk, :NV], val_pair)
        shifted[chunk, :] = (both[:, :NVEC] + both[:, NVEC:]) - filter_center
        return carry

    lax.fori_loop(0, NPC, make_shifted, 0)
    mix_load.wait()

    def mixed_of(total):
        for b in range(NB):
            total.done(b)
            for h in range(2):
                at = b * MB + h * 128
                piece = total.whole[b, h * 16 : (h + 1) * 16].reshape(NVEC, 128).T
                high, low = halves(piece)
                mixed_pair[at : at + 128, :NVEC] = high
                mixed_pair[at : at + 128, NVEC:] = low
        both = dot(mix[...], mixed_pair[...])
        high, low = halves(both[:, :NVEC] + both[:, NVEC:])
        mixed_pair[:, :NVEC] = high
        mixed_pair[:, NVEC:] = low

    def expand(chunk):
        both = dot(rows[chunk, :], mixed_pair[...])
        return both[:, :NVEC] + both[:, NVEC:]

    for b in range(NB // 2):
        sum1.to_gather(b)
    for b in range(NB // 2, NB):
        sum1.to_depth(b)
    for b in range(NB // 2, NB):
        sum1.to_gather(b)
    for b in range(NB):
        sum1.to_join(b)
    mixed_of(sum1)

    def first_step(j, carry):
        chunk = pl.ds(pl.multiple_of(j * PC, PC), PC)
        before = pl.ds(pl.multiple_of(jnp.maximum(j - 1, 0) * PC, PC), PC)
        so_far = gathered[...] + project(before, slice(None))
        gathered[...] = jnp.where(j > 0, so_far, 0.0)
        value = shifted[chunk, :] * trial[chunk, :].astype(F32) + expand(chunk)
        rounded = (value * (1.0 / filter_half)).astype(BF16)
        first_out[chunk, :] = rounded
        turned[:, chunk] = rounded.astype(F32).T.astype(BF16)
        return carry

    lax.fori_loop(0, NPC, first_step, 0)
    keep(sum2, 0, gathered[...] + project(slice(PAIRS - PC, PAIRS), slice(None)))
    for b in range(NB):
        sum2.to_core(b)
    for b in range(NB):
        sum2.to_plane(b)
    for b in range(NB):
        sum2.to_depth(b)
    for b in range(NB):
        sum2.to_gather(b)
    for b in range(NB):
        sum2.to_join(b)
    mixed_of(sum2)

    def second_step(j, carry):
        chunk = pl.ds(pl.multiple_of(j * PC, PC), PC)
        value = shifted[chunk, :] * first_out[chunk, :].astype(F32) + expand(chunk)
        filtered_out[chunk, :] = value * (2.0 / filter_half) - trial[chunk, :].astype(F32)
        return carry

    lax.fori_loop(0, NPC, second_step, 0)
    sum1.close()
    sum2.close()


def store_kernel(first_in, filtered_in, first_out, filtered_out, sem):
    copies = [
        pltpu.make_async_copy(first_in, first_out, sem.at[0]),
        pltpu.make_async_copy(filtered_in, filtered_out, sem.at[1]),
    ]
    for copy in copies:
        copy.start()
    for copy in copies:
        copy.wait()


def shards(
    val_orb, con_orb, val_energy, con_energy, points, val_band, con_band, kernel, trial_vecs
):
    vmem = pl.BlockSpec(memory_space=pltpu.VMEM)
    away = pl.BlockSpec(memory_space=pltpu.HBM)

    def sum_buffers():
        return [
            pltpu.VMEM((NB, MB, NVEC), F32),
            pltpu.VMEM((NB, 128, NVEC), F32),
            pltpu.VMEM((NB, 16, 8, NVEC), F32),
            pltpu.VMEM((NB, 16, 8, NVEC), F32),
            pltpu.VMEM((NB, 8, 8, NVEC), F32),
            pltpu.VMEM((NB, 32, 8, NVEC), F32),
        ]

    shapes = (
        jax.ShapeDtypeStruct((PAIRS, NVEC), BF16),
        jax.ShapeDtypeStruct((PAIRS, NVEC), F32),
    )
    first, filtered = pl.pallas_call(
        filter_kernel,
        out_shape=shapes,
        in_specs=[away] * 9,
        out_specs=(vmem, vmem),
        scratch_shapes=[
            pltpu.VMEM((1, NV), F32),
            pltpu.VMEM((1, NC), F32),
            pltpu.VMEM((8, 128), jnp.int32),
            pltpu.VMEM((PAIRS // 128, 128), jnp.int32),
            pltpu.VMEM((PAIRS // 128, 128), jnp.int32),
            pltpu.VMEM((NC + NV, NGRID), BF16),
            pltpu.VMEM((PAIRS, NC), BF16),
            pltpu.VMEM((PAIRS, 128), BF16),
            pltpu.VMEM((NCB, NGRID, CB), BF16),
            pltpu.VMEM((NC + 128, CB), BF16),
            pltpu.VMEM((PAIRS, NMU), BF16),
            pltpu.VMEM((PAIRS, NVEC), BF16),
            pltpu.VMEM((NVEC, PAIRS), BF16),
            pltpu.VMEM((NVEC, NMU), F32),
            pltpu.VMEM((NMU, NMU), BF16),
            pltpu.VMEM((PAIRS, NVEC), F32),
            pltpu.VMEM((NMU, 2 * NVEC), BF16),
        ]
        + sum_buffers()
        + sum_buffers()
        + [
            pltpu.SemaphoreType.DMA((9,)),
            pltpu.SemaphoreType.DMA((5,)),
            pltpu.SemaphoreType.DMA((5, NB)),
            pltpu.SemaphoreType.DMA((5,)),
            pltpu.SemaphoreType.DMA((5, NB)),
        ],
        compiler_params=pltpu.CompilerParams(
            collective_id=0, has_side_effects=True, vmem_limit_bytes=48 * 1024 * 1024
        ),
    )(
        *(
            pltpu.with_memory_space_constraint(value, pltpu.HBM)
            for value in (
                val_orb,
                con_orb,
                val_energy.reshape(1, NV),
                con_energy.reshape(1, NC),
                points.reshape(8, 128),
                val_band.reshape(PAIRS // 128, 128),
                con_band.reshape(PAIRS // 128, 128),
                kernel,
                trial_vecs,
            )
        )
    )
    return pl.pallas_call(
        store_kernel,
        out_shape=shapes,
        in_specs=[vmem, vmem],
        out_specs=(away, away),
        scratch_shapes=[pltpu.SemaphoreType.DMA((2,))],
        compiler_params=pltpu.CompilerParams(vmem_limit_bytes=1024 * 1024),
    )(first, filtered)


def solution(mesh):
    placed = (P(), P(), P(), P(), P(), P(("row", "col")), P(("row", "col")), P(), P(("row", "col"), None))
    return jax.shard_map(
        shards,
        mesh=mesh,
        in_specs=placed,
        out_specs=(P(("row", "col"), None), P(("row", "col"), None)),
        check_vma=False,
    )
```

```python
import jax
import jax.numpy as jnp
from jax import lax
from jax.experimental import pallas as pl
from jax.experimental.pallas import tpu as pltpu
from jax.sharding import PartitionSpec as P

filter_center = 2.25
filter_half = 1.25

F32 = jnp.float32
BF16 = jnp.bfloat16
MESH = pl.DeviceIdType.MESH

NMU, NVEC, NV, NC, NGRID = 1024, 128, 64, 512, 2048
PAIRS = 4096
NB = 4
MB = NMU // NB
NCB = 2
CB = NMU // NCB
PF = 1024
NPF = PAIRS // PF
PL = 1024
NPL = PAIRS // PL
PE = 1024
PR = 1024
NPR = PAIRS // PR

CORE, PLANE, DEPTH, GATHER, JOIN = range(5)
PLANE_STEPS = sorted(
    range(1, 16), key=lambda d: -(min(d // 4, 4 - d // 4) + min(d % 4, 4 - d % 4))
)
DEPTH_STEPS = sorted(range(1, 8), key=lambda d: -min(d, 8 - d))


def dot(a, b):
    return jnp.dot(a, b, preferred_element_type=F32)


def halves(wide):
    high = wide.astype(BF16)
    low = (wide - high.astype(F32)).astype(BF16)
    return high, low


class Place:
    def __init__(self):
        row, col = lax.axis_index("row"), lax.axis_index("col")
        self.core = lax.rem(row, 2)
        self.x = lax.rem(lax.div(row, 2), 4)
        self.y = lax.div(col, 8) * 2 + lax.div(row, 8)
        self.z = lax.rem(col, 8)

    def at(self, x, y, z, core):
        row = (lax.rem(y, 2) * 4 + x) * 2 + core
        col = lax.div(y, 2) * 8 + z
        return (row, col)

    def partner(self):
        return self.at(self.x, self.y, self.z, 1 - self.core)

    def plane(self, d):
        x = lax.rem(self.x + d % 4, 4)
        y = lax.rem(self.y + d // 4, 4)
        return self.at(x, y, self.z, self.core)

    def depth(self, d):
        return self.at(self.x, self.y, lax.rem(self.z + d, 8), self.core)

    def everyone(self):
        return (
            [self.partner()]
            + [self.plane(d) for d in PLANE_STEPS]
            + [self.depth(d) for d in DEPTH_STEPS]
        )


class Sum:
    def __init__(self, place, part, core_in, half, plane_in, depth_in, whole, send, recv):
        self.p = place
        self.part, self.core_in, self.half = part, core_in, half
        self.plane_in, self.depth_in, self.whole = plane_in, depth_in, whole
        self.send, self.recv = send, recv
        self.slot = place.y * 4 + place.x
        self.owner = place.core * 16 + self.slot

    def copy(self, src, dst, stage, b, device):
        pltpu.make_async_remote_copy(
            src_ref=src,
            dst_ref=dst,
            send_sem=self.send.at[stage],
            recv_sem=self.recv.at[stage, b],
            device_id=device,
            device_id_type=MESH,
        ).start()

    def arrived(self, ref, stage, b):
        pltpu.make_async_copy(ref, ref, self.recv.at[stage, b]).wait()

    def sent(self, ref, stage):
        pltpu.make_async_copy(ref, ref, self.send.at[stage]).wait()

    def to_core(self, b):
        other = pl.multiple_of((1 - self.p.core) * 128, 128)
        self.copy(self.part.at[b, pl.ds(other, 128)], self.core_in.at[b], CORE, b, self.p.partner())

    def to_plane(self, b):
        self.arrived(self.core_in.at[b], CORE, b)
        own = pl.multiple_of(self.p.core * 128, 128)
        both = self.part[b, pl.ds(own, 128), :] + self.core_in[b]
        self.half[b] = both.reshape(16, 8, NVEC)
        for d in PLANE_STEPS:
            x = lax.rem(self.p.x + d % 4, 4)
            y = lax.rem(self.p.y + d // 4, 4)
            self.copy(self.half.at[b, y * 4 + x], self.plane_in.at[b, d], PLANE, b, self.p.plane(d))

    def to_depth(self, b):
        self.arrived(self.plane_in.at[b, pl.ds(1, 15)], PLANE, b)
        total = self.half[b, self.slot]
        for d in range(1, 16):
            total = total + self.plane_in[b, d]
        self.depth_in[b, 0] = total
        for d in DEPTH_STEPS:
            self.copy(self.depth_in.at[b, 0], self.depth_in.at[b, d], DEPTH, b, self.p.depth(d))

    def to_gather(self, b):
        self.arrived(self.depth_in.at[b, pl.ds(1, 7)], DEPTH, b)
        total = self.depth_in[b, 0]
        for d in range(1, 8):
            total = total + self.depth_in[b, d]
        self.whole[b, self.owner] = total
        for d in PLANE_STEPS:
            piece = self.whole.at[b, self.owner]
            self.copy(piece, piece, GATHER, b, self.p.plane(d))

    def to_join(self, b):
        self.arrived(self.plane_in.at[b, pl.ds(1, 15)], GATHER, b)
        piece = self.whole.at[b, pl.ds(self.p.core * 16, 16)]
        self.copy(piece, piece, JOIN, b, self.p.partner())

    def done(self, b):
        self.arrived(self.whole.at[b, pl.ds(0, 16)], JOIN, b)

    def close(self):
        self.sent(self.core_in, CORE)
        self.sent(self.plane_in.at[:, pl.ds(1, 15)], PLANE)
        self.sent(self.depth_in.at[:, pl.ds(1, 7)], DEPTH)
        self.sent(self.plane_in.at[:, pl.ds(1, 15)], GATHER)
        self.sent(self.whole.at[:, pl.ds(0, 16)], JOIN)


def filter_kernel(
    val_hbm, con_hbm, val_energy_hbm, con_energy_hbm, points_hbm, val_band_hbm, con_band_hbm,
    kernel_hbm, trial_hbm,
    first_out, rows, trial, shifted, mixed_pair,
    val_energy, con_energy, points, val_band, con_band,
    orb, con_hot, val_hot, grid_hot, points_rows, turned, gathered, mix,
    part1, core1, half1, plane1, depth1, whole1,
    part2, core2, half2, plane2, depth2, whole2,
    load_sem, send1, recv1, send2, recv2,
):
    def load(src, dst, k):
        copy = pltpu.make_async_copy(src, dst, load_sem.at[k])
        copy.start()
        return copy

    points_load = load(points_hbm, points, 0)
    con_band_load = load(con_band_hbm, con_band, 1)
    val_band_load = load(val_band_hbm, val_band, 2)
    con_load = load(con_hbm, orb.at[pl.ds(0, NC)], 3)
    val_load = load(val_hbm, orb.at[pl.ds(NC, NV)], 4)
    trial_load = load(trial_hbm, trial, 5)
    con_energy_load = load(con_energy_hbm, con_energy, 6)
    val_energy_load = load(val_energy_hbm, val_energy, 7)
    mix_load = load(kernel_hbm, mix, 8)

    place = Place()
    barrier = pltpu.get_barrier_semaphore()
    for device in place.everyone():
        pl.semaphore_signal(barrier, inc=1, device_id=device, device_id_type=MESH)

    def build_grid(b, t):
        ids = lax.broadcasted_iota(jnp.int32, (128, 128), 0) + t * 128
        for j in range(CB // 128):
            k = b * (CB // 128) + j
            grid_hot[b, pl.ds(pl.multiple_of(t * 128, 128), 128), j * 128 : (j + 1) * 128] = jnp.where(
                ids == points[k : k + 1, :], 1.0, 0.0
            ).astype(BF16)

    def build_first_grid(t, carry):
        build_grid(0, t)
        build_grid(1, t)
        return carry

    points_load.wait()
    lax.fori_loop(0, NGRID // 128, build_first_grid, 0)
    con_band_load.wait()
    val_band_load.wait()

    def build_hot(j):
        both = (con_band[pl.ds(j, 1), :] * NV + val_band[pl.ds(j, 1), :]).astype(F32)
        column = jnp.broadcast_to(both, (128, 128)).T.astype(jnp.int32)
        con_column = lax.shift_right_logical(column, 6)
        val_column = lax.bitwise_and(column, NV - 1)
        ids = lax.broadcasted_iota(jnp.int32, (128, 128), 1)
        pairs = pl.ds(pl.multiple_of(j * 128, 128), 128)
        for t in range(NC // 128):
            con_hot[pairs, t * 128 : (t + 1) * 128] = jnp.where(ids + t * 128 == con_column, 1.0, 0.0).astype(BF16)
        val_hot[pairs, :] = jnp.where(ids == val_column, 1.0, 0.0).astype(BF16)

    con_load.wait()
    val_load.wait()

    sum1 = Sum(place, part1, core1, half1, plane1, depth1, whole1, send1, recv1)
    sum2 = Sum(place, part2, core2, half2, plane2, depth2, whole2, send2, recv2)

    def project(chunk, lanes):
        return dot(turned[:, chunk], rows[chunk, lanes])

    def keep(total, first, value):
        for k in range(value.shape[1] // 128):
            b, h = first + k // 2, k % 2
            total.part[b, h * 128 : (h + 1) * 128, :] = value[:, k * 128 : (k + 1) * 128]

    points_rows[NC + NV :, :] = jnp.zeros((128 - NV, CB), BF16)
    for c in range(NCB):
        steps = 4 if c == 0 else 2
        height = (NC + NV) // steps

        def pick_points(j, carry):
            some = pl.ds(pl.multiple_of(j * height, height), height)
            points_rows[some, :] = dot(orb[some, :], grid_hot[c]).astype(BF16)
            if c == 0:
                for k in range(PAIRS // 128 // steps):
                    build_hot(j * (PAIRS // 128 // steps) + k)
            return carry

        lax.fori_loop(0, steps, pick_points, 0)
        if c == 0:
            trial_load.wait()
        if c == 1:
            for b in range(NB // 2):
                sum1.to_plane(b)
        block = slice(c * CB, (c + 1) * CB)

        def make_rows(j, carry):
            chunk = pl.ds(pl.multiple_of(j * PR, PR), PR)
            before = pl.ds(pl.multiple_of(jnp.maximum(j - 1, 0) * PR, PR), PR)
            so_far = gathered[:, :CB] + project(before, block)
            gathered[:, :CB] = jnp.where(j > 0, so_far, 0.0)
            con_part = dot(con_hot[chunk, :], points_rows[:NC, :])
            val_part = dot(val_hot[chunk, :], points_rows[NC:, :])
            rows[chunk, block] = (con_part * val_part).astype(BF16)
            if c == 0:
                turned[:, chunk] = trial[chunk, :].astype(F32).T.astype(BF16)
            return carry

        lax.fori_loop(0, NPR, make_rows, 0)
        keep(sum1, c * 2, gathered[:, :CB] + project(slice(PAIRS - PR, PAIRS), block))
        if c == 0:
            pl.semaphore_wait(barrier, 23)
        sum1.to_core(c * 2)
        sum1.to_core(c * 2 + 1)

    for b in range(NB // 2):
        sum1.to_depth(b)
    for b in range(NB // 2, NB):
        sum1.to_plane(b)
    con_energy_load.wait()
    val_energy_load.wait()
    con_col = jnp.broadcast_to(con_energy[...], (128, NC)).T
    val_col = jnp.broadcast_to(val_energy[...], (128, NV)).T
    con_pair = jnp.concatenate(halves(con_col), axis=1)
    val_pair = jnp.concatenate(halves(-val_col), axis=1)

    def make_shifted(j, carry):
        chunk = pl.ds(pl.multiple_of(j * PE, PE), PE)
        both = dot(con_hot[chunk, :], con_pair) + dot(val_hot[chunk, :NV], val_pair)
        shifted[chunk, :] = (both[:, :NVEC] + both[:, NVEC:]) - filter_center
        return carry

    lax.fori_loop(0, PAIRS // PE, make_shifted, 0)
    mix_load.wait()

    def mixed_of(total):
        for b in range(NB):
            total.done(b)
            for h in range(2):
                at = b * MB + h * 128
                piece = total.whole[b, h * 16 : (h + 1) * 16].reshape(NVEC, 128).T
                high, low = halves(piece)
                mixed_pair[at : at + 128, :NVEC] = high
                mixed_pair[at : at + 128, NVEC:] = low
        both = dot(mix[...], mixed_pair[...])
        high, low = halves(both[:, :NVEC] + both[:, NVEC:])
        mixed_pair[:, :NVEC] = high
        mixed_pair[:, NVEC:] = low

    def expand(chunk):
        both = dot(rows[chunk, :], mixed_pair[...])
        return both[:, :NVEC] + both[:, NVEC:]

    for b in range(NB // 2):
        sum1.to_gather(b)
    for b in range(NB // 2, NB):
        sum1.to_depth(b)
    for b in range(NB // 2, NB):
        sum1.to_gather(b)
    for b in range(NB):
        sum1.to_join(b)
    mixed_of(sum1)

    def first_step(j, carry):
        chunk = pl.ds(pl.multiple_of(j * PF, PF), PF)
        before = pl.ds(pl.multiple_of(jnp.maximum(j - 1, 0) * PF, PF), PF)
        so_far = gathered[...] + project(before, slice(None))
        gathered[...] = jnp.where(j > 0, so_far, 0.0)
        value = shifted[chunk, :] * trial[chunk, :].astype(F32) + expand(chunk)
        rounded = (value * (1.0 / filter_half)).astype(BF16)
        first_out[chunk, :] = rounded
        turned[:, chunk] = rounded.astype(F32).T.astype(BF16)
        return carry

    lax.fori_loop(0, NPF, first_step, 0)
    keep(sum2, 0, gathered[...] + project(slice(PAIRS - PF, PAIRS), slice(None)))
    for b in range(NB):
        sum2.to_core(b)
    for b in range(NB):
        sum2.to_plane(b)
    for b in range(NB):
        sum2.to_depth(b)
    for b in range(NB):
        sum2.to_gather(b)
    for b in range(NB):
        sum2.to_join(b)
    mixed_of(sum2)

    sum1.close()
    sum2.close()


def last_kernel(first_in, rows, trial, shifted, mixed_pair, first_out, filtered_out, filtered, sem):
    first_copy = pltpu.make_async_copy(first_in, first_out, sem.at[NPL])
    first_copy.start()

    def store(j, chunk):
        return pltpu.make_async_copy(filtered.at[chunk], filtered_out.at[chunk], sem.at[j])

    def second_step(j, carry):
        chunk = pl.ds(pl.multiple_of(j * PL, PL), PL)
        both = dot(rows[chunk, :], mixed_pair[...])
        value = shifted[chunk, :] * first_in[chunk, :].astype(F32) + (both[:, :NVEC] + both[:, NVEC:])
        filtered[chunk, :] = value * (2.0 / filter_half) - trial[chunk, :].astype(F32)
        store(j, chunk).start()
        return carry

    lax.fori_loop(0, NPL, second_step, 0)
    for j in range(NPL):
        store(j, slice(j * PL, (j + 1) * PL)).wait()
    first_copy.wait()


def shards(
    val_orb, con_orb, val_energy, con_energy, points, val_band, con_band, kernel, trial_vecs
):
    vmem = pl.BlockSpec(memory_space=pltpu.VMEM)
    away = pl.BlockSpec(memory_space=pltpu.HBM)

    def sum_buffers():
        return [
            pltpu.VMEM((NB, MB, NVEC), F32),
            pltpu.VMEM((NB, 128, NVEC), F32),
            pltpu.VMEM((NB, 16, 8, NVEC), F32),
            pltpu.VMEM((NB, 16, 8, NVEC), F32),
            pltpu.VMEM((NB, 8, 8, NVEC), F32),
            pltpu.VMEM((NB, 32, 8, NVEC), F32),
        ]

    shapes = (
        jax.ShapeDtypeStruct((PAIRS, NVEC), BF16),
        jax.ShapeDtypeStruct((PAIRS, NVEC), F32),
    )
    kept = pl.pallas_call(
        filter_kernel,
        out_shape=(
            jax.ShapeDtypeStruct((PAIRS, NVEC), BF16),
            jax.ShapeDtypeStruct((PAIRS, NMU), BF16),
            jax.ShapeDtypeStruct((PAIRS, NVEC), BF16),
            jax.ShapeDtypeStruct((PAIRS, NVEC), F32),
            jax.ShapeDtypeStruct((NMU, 2 * NVEC), BF16),
        ),
        in_specs=[away] * 9,
        out_specs=(vmem,) * 5,
        scratch_shapes=[
            pltpu.VMEM((1, NV), F32),
            pltpu.VMEM((1, NC), F32),
            pltpu.VMEM((8, 128), jnp.int32),
            pltpu.VMEM((PAIRS // 128, 128), jnp.int32),
            pltpu.VMEM((PAIRS // 128, 128), jnp.int32),
            pltpu.VMEM((NC + NV, NGRID), BF16),
            pltpu.VMEM((PAIRS, NC), BF16),
            pltpu.VMEM((PAIRS, 128), BF16),
            pltpu.VMEM((NCB, NGRID, CB), BF16),
            pltpu.VMEM((NC + 128, CB), BF16),
            pltpu.VMEM((NVEC, PAIRS), BF16),
            pltpu.VMEM((NVEC, NMU), F32),
            pltpu.VMEM((NMU, NMU), BF16),
        ]
        + sum_buffers()
        + sum_buffers()
        + [
            pltpu.SemaphoreType.DMA((9,)),
            pltpu.SemaphoreType.DMA((5,)),
            pltpu.SemaphoreType.DMA((5, NB)),
            pltpu.SemaphoreType.DMA((5,)),
            pltpu.SemaphoreType.DMA((5, NB)),
        ],
        compiler_params=pltpu.CompilerParams(
            collective_id=0, has_side_effects=True, vmem_limit_bytes=36 * 1024 * 1024
        ),
    )(
        *(
            pltpu.with_memory_space_constraint(value, pltpu.HBM)
            for value in (
                val_orb,
                con_orb,
                val_energy.reshape(1, NV),
                con_energy.reshape(1, NC),
                points.reshape(8, 128),
                val_band.reshape(PAIRS // 128, 128),
                con_band.reshape(PAIRS // 128, 128),
                kernel,
                trial_vecs,
            )
        )
    )
    return pl.pallas_call(
        last_kernel,
        out_shape=shapes,
        in_specs=[vmem] * 5,
        out_specs=(away, away),
        scratch_shapes=[pltpu.VMEM((PAIRS, NVEC), F32), pltpu.SemaphoreType.DMA((NPL + 1,))],
        compiler_params=pltpu.CompilerParams(vmem_limit_bytes=8 * 1024 * 1024),
    )(*kept)


def solution(mesh):
    placed = (P(), P(), P(), P(), P(), P(("row", "col")), P(("row", "col")), P(), P(("row", "col"), None))
    return jax.shard_map(
        shards,
        mesh=mesh,
        in_specs=placed,
        out_specs=(P(("row", "col"), None), P(("row", "col"), None)),
        check_vma=False,
    )
```

```python
import jax
import jax.numpy as jnp
from jax import lax
from jax.experimental import pallas as pl
from jax.experimental.pallas import tpu as pltpu
from jax.sharding import PartitionSpec as P

filter_center = 2.25
filter_half = 1.25

F32 = jnp.float32
BF16 = jnp.bfloat16
MESH = pl.DeviceIdType.MESH

NMU, NVEC, NV, NC, NGRID = 1024, 128, 64, 512, 2048
PAIRS = 4096
NB = 4
MB = NMU // NB
NCB = 2
CB = NMU // NCB
PF = 2048
NPF = PAIRS // PF
PL = 2048
NPL = PAIRS // PL
PE = 1024
PR = 2048
NPR = PAIRS // PR

CORE, PLANE, DEPTH, GATHER, JOIN = range(5)
PLANE_STEPS = sorted(
    range(1, 16), key=lambda d: -(min(d // 4, 4 - d // 4) + min(d % 4, 4 - d % 4))
)
DEPTH_STEPS = sorted(range(1, 8), key=lambda d: -min(d, 8 - d))


def dot(a, b):
    return jnp.dot(a, b, preferred_element_type=F32)


def halves(wide):
    high = wide.astype(BF16)
    low = (wide - high.astype(F32)).astype(BF16)
    return high, low


class Place:
    def __init__(self):
        row, col = lax.axis_index("row"), lax.axis_index("col")
        self.core = lax.rem(row, 2)
        self.x = lax.rem(lax.div(row, 2), 4)
        self.y = lax.div(col, 8) * 2 + lax.div(row, 8)
        self.z = lax.rem(col, 8)

    def at(self, x, y, z, core):
        row = (lax.rem(y, 2) * 4 + x) * 2 + core
        col = lax.div(y, 2) * 8 + z
        return (row, col)

    def partner(self):
        return self.at(self.x, self.y, self.z, 1 - self.core)

    def plane(self, d):
        x = lax.rem(self.x + d % 4, 4)
        y = lax.rem(self.y + d // 4, 4)
        return self.at(x, y, self.z, self.core)

    def depth(self, d):
        return self.at(self.x, self.y, lax.rem(self.z + d, 8), self.core)

    def everyone(self):
        return (
            [self.partner()]
            + [self.plane(d) for d in PLANE_STEPS]
            + [self.depth(d) for d in DEPTH_STEPS]
        )


class Sum:
    def __init__(self, place, part, core_in, half, plane_in, depth_in, whole, send, recv):
        self.p = place
        self.part, self.core_in, self.half = part, core_in, half
        self.plane_in, self.depth_in, self.whole = plane_in, depth_in, whole
        self.send, self.recv = send, recv
        self.slot = place.y * 4 + place.x
        self.owner = place.core * 16 + self.slot

    def copy(self, src, dst, stage, b, device):
        pltpu.make_async_remote_copy(
            src_ref=src,
            dst_ref=dst,
            send_sem=self.send.at[stage],
            recv_sem=self.recv.at[stage, b],
            device_id=device,
            device_id_type=MESH,
        ).start()

    def arrived(self, ref, stage, b):
        pltpu.make_async_copy(ref, ref, self.recv.at[stage, b]).wait()

    def sent(self, ref, stage):
        pltpu.make_async_copy(ref, ref, self.send.at[stage]).wait()

    def to_core(self, b):
        other = pl.multiple_of((1 - self.p.core) * 128, 128)
        self.copy(self.part.at[b, pl.ds(other, 128)], self.core_in.at[b], CORE, b, self.p.partner())

    def to_plane(self, b):
        self.arrived(self.core_in.at[b], CORE, b)
        own = pl.multiple_of(self.p.core * 128, 128)
        both = self.part[b, pl.ds(own, 128), :] + self.core_in[b]
        self.half[b] = both.reshape(16, 8, NVEC)
        for d in PLANE_STEPS:
            x = lax.rem(self.p.x + d % 4, 4)
            y = lax.rem(self.p.y + d // 4, 4)
            self.copy(self.half.at[b, y * 4 + x], self.plane_in.at[b, d], PLANE, b, self.p.plane(d))

    def to_depth(self, b):
        self.arrived(self.plane_in.at[b, pl.ds(1, 15)], PLANE, b)
        total = self.half[b, self.slot]
        for d in range(1, 16):
            total = total + self.plane_in[b, d]
        self.depth_in[b, 0] = total
        for d in DEPTH_STEPS:
            self.copy(self.depth_in.at[b, 0], self.depth_in.at[b, d], DEPTH, b, self.p.depth(d))

    def to_gather(self, b):
        self.arrived(self.depth_in.at[b, pl.ds(1, 7)], DEPTH, b)
        total = self.depth_in[b, 0]
        for d in range(1, 8):
            total = total + self.depth_in[b, d]
        self.whole[b, self.owner] = total
        for d in PLANE_STEPS:
            piece = self.whole.at[b, self.owner]
            self.copy(piece, piece, GATHER, b, self.p.plane(d))

    def to_join(self, b):
        self.arrived(self.plane_in.at[b, pl.ds(1, 15)], GATHER, b)
        piece = self.whole.at[b, pl.ds(self.p.core * 16, 16)]
        self.copy(piece, piece, JOIN, b, self.p.partner())

    def done(self, b):
        self.arrived(self.whole.at[b, pl.ds(0, 16)], JOIN, b)

    def close(self):
        self.sent(self.core_in, CORE)
        self.sent(self.plane_in.at[:, pl.ds(1, 15)], PLANE)
        self.sent(self.depth_in.at[:, pl.ds(1, 7)], DEPTH)
        self.sent(self.plane_in.at[:, pl.ds(1, 15)], GATHER)
        self.sent(self.whole.at[:, pl.ds(0, 16)], JOIN)


def filter_kernel(
    val_hbm, con_hbm, val_energy_hbm, con_energy_hbm, points_hbm, val_band_hbm, con_band_hbm,
    kernel_hbm, trial_hbm,
    first_out, rows, trial, shifted, mixed_pair,
    val_energy, con_energy, points, val_band, con_band,
    orb, con_hot, val_hot, grid_hot, points_rows, turned, gathered, mix,
    part1, core1, half1, plane1, depth1, whole1,
    part2, core2, half2, plane2, depth2, whole2,
    load_sem, send1, recv1, send2, recv2,
):
    def load(src, dst, k):
        copy = pltpu.make_async_copy(src, dst, load_sem.at[k])
        copy.start()
        return copy

    points_load = load(points_hbm, points, 0)
    con_band_load = load(con_band_hbm, con_band, 1)
    val_band_load = load(val_band_hbm, val_band, 2)
    con_load = load(con_hbm, orb.at[pl.ds(0, NC)], 3)
    val_load = load(val_hbm, orb.at[pl.ds(NC, NV)], 4)
    trial_load = load(trial_hbm, trial, 5)
    con_energy_load = load(con_energy_hbm, con_energy, 6)
    val_energy_load = load(val_energy_hbm, val_energy, 7)
    mix_load = load(kernel_hbm, mix, 8)

    place = Place()
    barrier = pltpu.get_barrier_semaphore()
    for device in place.everyone():
        pl.semaphore_signal(barrier, inc=1, device_id=device, device_id_type=MESH)

    def build_grid(b, t):
        ids = lax.broadcasted_iota(jnp.int32, (128, 128), 0) + t * 128
        for j in range(CB // 128):
            k = b * (CB // 128) + j
            grid_hot[b, pl.ds(pl.multiple_of(t * 128, 128), 128), j * 128 : (j + 1) * 128] = jnp.where(
                ids == points[k : k + 1, :], 1.0, 0.0
            ).astype(BF16)

    def build_first_grid(t, carry):
        build_grid(0, t)
        build_grid(1, t)
        return carry

    points_load.wait()
    lax.fori_loop(0, NGRID // 128, build_first_grid, 0)
    con_band_load.wait()
    val_band_load.wait()

    def build_hot(j):
        both = (con_band[pl.ds(j, 1), :] * NV + val_band[pl.ds(j, 1), :]).astype(F32)
        column = jnp.broadcast_to(both, (128, 128)).T.astype(jnp.int32)
        con_column = lax.shift_right_logical(column, 6)
        val_column = lax.bitwise_and(column, NV - 1)
        ids = lax.broadcasted_iota(jnp.int32, (128, 128), 1)
        pairs = pl.ds(pl.multiple_of(j * 128, 128), 128)
        for t in range(NC // 128):
            con_hot[pairs, t * 128 : (t + 1) * 128] = jnp.where(ids + t * 128 == con_column, 1.0, 0.0).astype(BF16)
        val_hot[pairs, :] = jnp.where(ids == val_column, 1.0, 0.0).astype(BF16)

    con_load.wait()
    val_load.wait()

    sum1 = Sum(place, part1, core1, half1, plane1, depth1, whole1, send1, recv1)
    sum2 = Sum(place, part2, core2, half2, plane2, depth2, whole2, send2, recv2)

    def project(chunk, lanes):
        return dot(turned[:, chunk], rows[chunk, lanes])

    def keep(total, first, value):
        for k in range(value.shape[1] // 128):
            b, h = first + k // 2, k % 2
            total.part[b, h * 128 : (h + 1) * 128, :] = value[:, k * 128 : (k + 1) * 128]

    points_rows[NC + NV :, :] = jnp.zeros((128 - NV, CB), BF16)
    for c in range(NCB):
        steps = 2 if c == 0 else 1
        height = (NC + NV) // steps

        def pick_points(j, carry):
            some = pl.ds(pl.multiple_of(j * height, height), height)
            points_rows[some, :] = dot(orb[some, :], grid_hot[c]).astype(BF16)
            if c == 0:
                for k in range(PAIRS // 128 // steps):
                    build_hot(j * (PAIRS // 128 // steps) + k)
            return carry

        lax.fori_loop(0, steps, pick_points, 0)
        if c == 0:
            trial_load.wait()
        if c == 1:
            for b in range(NB // 2):
                sum1.to_plane(b)
        block = slice(c * CB, (c + 1) * CB)

        def make_rows(j, carry):
            chunk = pl.ds(pl.multiple_of(j * PR, PR), PR)
            before = pl.ds(pl.multiple_of(jnp.maximum(j - 1, 0) * PR, PR), PR)
            so_far = gathered[:, :CB] + project(before, block)
            gathered[:, :CB] = jnp.where(j > 0, so_far, 0.0)
            con_part = dot(con_hot[chunk, :], points_rows[:NC, :])
            val_part = dot(val_hot[chunk, :], points_rows[NC:, :])
            rows[chunk, block] = (con_part * val_part).astype(BF16)
            if c == 0:
                turned[:, chunk] = trial[chunk, :].astype(F32).T.astype(BF16)
            return carry

        lax.fori_loop(0, NPR, make_rows, 0)
        keep(sum1, c * 2, gathered[:, :CB] + project(slice(PAIRS - PR, PAIRS), block))
        if c == 0:
            pl.semaphore_wait(barrier, 23)
        sum1.to_core(c * 2)
        sum1.to_core(c * 2 + 1)

    for b in range(NB // 2):
        sum1.to_depth(b)
    for b in range(NB // 2, NB):
        sum1.to_plane(b)
    con_energy_load.wait()
    val_energy_load.wait()
    con_col = jnp.broadcast_to(con_energy[...], (128, NC)).T
    val_col = jnp.broadcast_to(val_energy[...], (128, NV)).T
    con_pair = jnp.concatenate(halves(con_col), axis=1)
    val_pair = jnp.concatenate(halves(-val_col), axis=1)

    def make_shifted(j, carry):
        chunk = pl.ds(pl.multiple_of(j * PE, PE), PE)
        both = dot(con_hot[chunk, :], con_pair) + dot(val_hot[chunk, :NV], val_pair)
        shifted[chunk, :] = (both[:, :NVEC] + both[:, NVEC:]) - filter_center
        return carry

    lax.fori_loop(0, PAIRS // PE, make_shifted, 0)
    mix_load.wait()

    def mixed_of(total):
        for b in range(NB):
            total.done(b)
            for h in range(2):
                at = b * MB + h * 128
                piece = total.whole[b, h * 16 : (h + 1) * 16].reshape(NVEC, 128).T
                high, low = halves(piece)
                mixed_pair[at : at + 128, :NVEC] = high
                mixed_pair[at : at + 128, NVEC:] = low
        both = dot(mix[...], mixed_pair[...])
        high, low = halves(both[:, :NVEC] + both[:, NVEC:])
        mixed_pair[:, :NVEC] = high
        mixed_pair[:, NVEC:] = low

    def expand(chunk):
        both = dot(rows[chunk, :], mixed_pair[...])
        return both[:, :NVEC] + both[:, NVEC:]

    for b in range(NB // 2):
        sum1.to_gather(b)
    for b in range(NB // 2, NB):
        sum1.to_depth(b)
    for b in range(NB // 2, NB):
        sum1.to_gather(b)
    for b in range(NB):
        sum1.to_join(b)
    mixed_of(sum1)

    def first_step(j, carry):
        chunk = pl.ds(pl.multiple_of(j * PF, PF), PF)
        before = pl.ds(pl.multiple_of(jnp.maximum(j - 1, 0) * PF, PF), PF)
        so_far = gathered[...] + project(before, slice(None))
        gathered[...] = jnp.where(j > 0, so_far, 0.0)
        value = shifted[chunk, :] * trial[chunk, :].astype(F32) + expand(chunk)
        rounded = (value * (1.0 / filter_half)).astype(BF16)
        first_out[chunk, :] = rounded
        turned[:, chunk] = rounded.astype(F32).T.astype(BF16)
        return carry

    lax.fori_loop(0, NPF, first_step, 0)
    keep(sum2, 0, gathered[...] + project(slice(PAIRS - PF, PAIRS), slice(None)))
    for b in range(NB):
        sum2.to_core(b)
    for b in range(NB):
        sum2.to_plane(b)
    for b in range(NB):
        sum2.to_depth(b)
    for b in range(NB):
        sum2.to_gather(b)
    for b in range(NB):
        sum2.to_join(b)
    mixed_of(sum2)

    sum1.close()
    sum2.close()


def last_kernel(first_in, rows, trial, shifted, mixed_pair, first_out, filtered_out, filtered, sem):
    first_copy = pltpu.make_async_copy(first_in, first_out, sem.at[NPL])
    first_copy.start()

    def store(j, chunk):
        return pltpu.make_async_copy(filtered.at[chunk], filtered_out.at[chunk], sem.at[j])

    def second_step(j, carry):
        chunk = pl.ds(pl.multiple_of(j * PL, PL), PL)
        both = dot(rows[chunk, :], mixed_pair[...])
        value = shifted[chunk, :] * first_in[chunk, :].astype(F32) + (both[:, :NVEC] + both[:, NVEC:])
        filtered[chunk, :] = value * (2.0 / filter_half) - trial[chunk, :].astype(F32)
        store(j, chunk).start()
        return carry

    lax.fori_loop(0, NPL, second_step, 0)
    for j in range(NPL):
        store(j, slice(j * PL, (j + 1) * PL)).wait()
    first_copy.wait()


def shards(
    val_orb, con_orb, val_energy, con_energy, points, val_band, con_band, kernel, trial_vecs
):
    vmem = pl.BlockSpec(memory_space=pltpu.VMEM)
    away = pl.BlockSpec(memory_space=pltpu.HBM)

    def sum_buffers():
        return [
            pltpu.VMEM((NB, MB, NVEC), F32),
            pltpu.VMEM((NB, 128, NVEC), F32),
            pltpu.VMEM((NB, 16, 8, NVEC), F32),
            pltpu.VMEM((NB, 16, 8, NVEC), F32),
            pltpu.VMEM((NB, 8, 8, NVEC), F32),
            pltpu.VMEM((NB, 32, 8, NVEC), F32),
        ]

    shapes = (
        jax.ShapeDtypeStruct((PAIRS, NVEC), BF16),
        jax.ShapeDtypeStruct((PAIRS, NVEC), F32),
    )
    kept = pl.pallas_call(
        filter_kernel,
        out_shape=(
            jax.ShapeDtypeStruct((PAIRS, NVEC), BF16),
            jax.ShapeDtypeStruct((PAIRS, NMU), BF16),
            jax.ShapeDtypeStruct((PAIRS, NVEC), BF16),
            jax.ShapeDtypeStruct((PAIRS, NVEC), F32),
            jax.ShapeDtypeStruct((NMU, 2 * NVEC), BF16),
        ),
        in_specs=[away] * 9,
        out_specs=(vmem,) * 5,
        scratch_shapes=[
            pltpu.VMEM((1, NV), F32),
            pltpu.VMEM((1, NC), F32),
            pltpu.VMEM((8, 128), jnp.int32),
            pltpu.VMEM((PAIRS // 128, 128), jnp.int32),
            pltpu.VMEM((PAIRS // 128, 128), jnp.int32),
            pltpu.VMEM((NC + NV, NGRID), BF16),
            pltpu.VMEM((PAIRS, NC), BF16),
            pltpu.VMEM((PAIRS, 128), BF16),
            pltpu.VMEM((NCB, NGRID, CB), BF16),
            pltpu.VMEM((NC + 128, CB), BF16),
            pltpu.VMEM((NVEC, PAIRS), BF16),
            pltpu.VMEM((NVEC, NMU), F32),
            pltpu.VMEM((NMU, NMU), BF16),
        ]
        + sum_buffers()
        + sum_buffers()
        + [
            pltpu.SemaphoreType.DMA((9,)),
            pltpu.SemaphoreType.DMA((5,)),
            pltpu.SemaphoreType.DMA((5, NB)),
            pltpu.SemaphoreType.DMA((5,)),
            pltpu.SemaphoreType.DMA((5, NB)),
        ],
        compiler_params=pltpu.CompilerParams(
            collective_id=0, has_side_effects=True, vmem_limit_bytes=36 * 1024 * 1024
        ),
    )(
        *(
            pltpu.with_memory_space_constraint(value, pltpu.HBM)
            for value in (
                val_orb,
                con_orb,
                val_energy.reshape(1, NV),
                con_energy.reshape(1, NC),
                points.reshape(8, 128),
                val_band.reshape(PAIRS // 128, 128),
                con_band.reshape(PAIRS // 128, 128),
                kernel,
                trial_vecs,
            )
        )
    )
    return pl.pallas_call(
        last_kernel,
        out_shape=shapes,
        in_specs=[vmem] * 5,
        out_specs=(away, away),
        scratch_shapes=[pltpu.VMEM((PAIRS, NVEC), F32), pltpu.SemaphoreType.DMA((NPL + 1,))],
        compiler_params=pltpu.CompilerParams(vmem_limit_bytes=8 * 1024 * 1024),
    )(*kept)


def solution(mesh):
    placed = (P(), P(), P(), P(), P(), P(("row", "col")), P(("row", "col")), P(), P(("row", "col"), None))
    return jax.shard_map(
        shards,
        mesh=mesh,
        in_specs=placed,
        out_specs=(P(("row", "col"), None), P(("row", "col"), None)),
        check_vma=False,
    )
```
